256 devices in a mesh: row: 16 (over y_hi, x, core), col: 16 (over y_lo, z).
Axes of the slice: x: 4, y: 4 (y_hi: 2, y_lo: 2; y = y_hi * 2 + y_lo), z: 8, core: 2. Of those that a mesh axis runs over, the one named last changes fastest.
Arguments:
- tokens: bfloat16 [8192, 6144], P('row', 'col'), may hold values from -6 to 6
- gate_weight: bfloat16 [6144, 12288], P('row', 'col'), may hold values from -0.078125 to 0.078125
- up_weight: bfloat16 [6144, 12288], P('row', 'col'), may hold values from -0.078125 to 0.078125
Outputs:
- hidden: float32 [8192, 12288], P('row', 'col')
The draws below stay inside these ranges and needn't reach their ends.
All inputs are finite; a program needn't handle non-finite values.
Results may differ from the reference program's by a relative error of at most 0.0003.
Values may be sent and summed in bfloat16 or wider, within the bound.
No kernel may reach another device: no remote copies, remote signals or barrier semaphores. Data moves between devices by JAX's collectives and lax.ppermute only.
A program may use at most 128 MiB of HBM per device.

```python
import jax
import jax.numpy as jnp

D = 6144
FFW = 12288
TOKENS = 8192


def block_scale(rng, dims, shards, low, largest):
    gain = 1.0
    for axis_at, shards_of in shards:
        steps = jax.random.uniform(jax.random.fold_in(jax.random.fold_in(rng, 6), axis_at), (shards_of,), jnp.float32, low / len(shards), largest / len(shards))
        gain = gain * jnp.repeat(jnp.exp(steps), dims[axis_at] // shards_of).reshape((-1,) + (1,) * (len(dims) - 1 - axis_at))
    return gain


def normal_values(rng, shape, width, limit, pieces=(), held_as=jnp.bfloat16):
    factor_of = block_scale(rng, shape, pieces, -0.22, 0.18) if pieces else 1.0
    drawn = jax.random.normal(rng, shape, jnp.float32) * width * factor_of
    return jnp.minimum(jnp.maximum(drawn, -limit), limit).astype(held_as)


def setup_inputs(seed: int = 0) -> dict:
    streams_of = jax.random.split(jax.random.key(seed), 4)
    tokens = normal_values(streams_of[0], (TOKENS, D), 1.0, 6.0, ((0, 16), (1, 16)))
    gate_weight = normal_values(streams_of[1], (D, FFW), D ** -0.5, 0.078125, ((0, 16), (1, 16)))
    up_weight = normal_values(streams_of[2], (D, FFW), D ** -0.5, 0.078125, ((0, 16), (1, 16)))
    return dict(tokens=tokens, gate_weight=gate_weight, up_weight=up_weight)


def reference(tokens, gate_weight, up_weight):
    gate_sum = jnp.dot(tokens, gate_weight, preferred_element_type=jnp.float32)
    up_sum = jnp.dot(tokens, up_weight, preferred_element_type=jnp.float32)
    return jax.nn.silu(gate_sum) * up_sum
```

```python
import functools

import jax
import jax.numpy as jnp
from jax import lax
from jax.experimental import pallas as pl
from jax.experimental.pallas import tpu as pltpu
from jax.sharding import Mesh
from jax.sharding import PartitionSpec as P

ROW = ("y_hi", "x", "core")
COL = ("y_lo", "z")


def shift(value, axis, size, by):
    return lax.ppermute(value, axis, [(i, (i + by) % size) for i in range(size)])


def multiply(origins, tokens_ref, *refs):
    y_hi, x, core = (lax.axis_index(name) for name in ROW)
    y_lo = lax.axis_index("y_lo")
    weights, hidden, tokens, held, gate, up, token_sem, weight_sem = refs[:16], *refs[16:]
    parts = len(weights) // 2
    depth = tokens_ref.shape[2]

    def token_copy(r, half):
        flip, offset = origins[r]
        from_core = core if half == 0 else 1 - core
        from_z = 2 * lax.rem(x + offset, 4) + from_core
        from_y = lax.rem(y_hi + flip + y_lo, 2)
        return pltpu.make_async_copy(
            tokens_ref.at[2 * from_z + from_y],
            tokens.at[r, :, pl.ds(half * depth, depth)],
            token_sem.at[r, half],
        )

    def weight_copy(r, half):
        return pltpu.make_async_copy(
            weights[2 * r + half],
            held.at[r, :, pl.ds(half * depth, depth), :],
            weight_sem.at[r, half],
        )

    for r in range(parts):
        for half in range(2):
            token_copy(r, half).start()
            weight_copy(r, half).start()
    for r in range(parts):
        for half in range(2):
            token_copy(r, half).wait()
            weight_copy(r, half).wait()
        gate_part = jnp.dot(tokens[r], held[r, 0], preferred_element_type=jnp.float32)
        up_part = jnp.dot(tokens[r], held[r, 1], preferred_element_type=jnp.float32)
        if r == 0:
            gate[...] = gate_part
            up[...] = up_part
        else:
            gate[...] += gate_part
            up[...] += up_part
    value = gate[...]
    hidden[...] = value / (1.0 + jnp.exp(-value)) * up[...]


def per_device(tokens, gate_weight, up_weight):
    rows, depth = tokens.shape
    width = gate_weight.shape[1]

    own = jnp.stack([gate_weight, up_weight])
    own, tokens = lax.optimization_barrier((own, tokens))
    other_tokens = shift(tokens, "y_lo", 2, 1)
    across = shift(own, "y_hi", 2, 1)
    own_2 = shift(own, "x", 4, 2)
    own_1 = shift(own, "x", 4, 1)
    own_3 = shift(own, "x", 4, -1)
    pair = jnp.stack([tokens, other_tokens])
    gathered = lax.all_gather(pair, "z", axis=0, tiled=True)
    across_1 = shift(across, "x", 4, 1)
    across_3 = shift(across, "x", 4, -1)
    across_2 = shift(own_2, "y_hi", 2, 1)

    blocks = [
        (0, 0, own),
        (0, 3, own_1),
        (0, 1, own_3),
        (0, 2, own_2),
        (1, 0, across),
        (1, 3, across_1),
        (1, 1, across_3),
        (1, 2, across_2),
    ]
    weights = []
    for _, _, block in blocks:
        weights += [block, shift(block, "core", 2, 1)]
    origins = tuple((flip, offset) for flip, offset, _ in blocks)
    parts = len(blocks)
    anywhere = pl.BlockSpec(memory_space=pl.ANY)
    return pl.pallas_call(
        functools.partial(multiply, origins),
        out_shape=jax.ShapeDtypeStruct((rows, width), jnp.float32),
        in_specs=[anywhere] * (1 + 2 * parts),
        out_specs=pl.BlockSpec(memory_space=pltpu.VMEM),
        scratch_shapes=[
            pltpu.VMEM((parts, rows, 2 * depth), tokens.dtype),
            pltpu.VMEM((parts, 2, 2 * depth, width), gate_weight.dtype),
            pltpu.VMEM((rows, width), jnp.float32),
            pltpu.VMEM((rows, width), jnp.float32),
            pltpu.SemaphoreType.DMA((parts, 2)),
            pltpu.SemaphoreType.DMA((parts, 2)),
        ],
        compiler_params=pltpu.CompilerParams(vmem_limit_bytes=48 * 1024 * 1024),
        cost_estimate=pl.CostEstimate(
            flops=4 * rows * width * depth * 16,
            bytes_accessed=2 * depth * 16 * (rows + 2 * width) + 4 * rows * width,
            transcendentals=rows * width,
        ),
    )(gathered, *weights)


def solution(mesh):
    fine = Mesh(mesh.devices.reshape(2, 4, 2, 2, 8), ROW + COL)
    spec = P(ROW, COL)
    return jax.shard_map(
        per_device, mesh=fine, in_specs=(spec,) * 3, out_specs=spec, check_vma=False
    )
```

```python
import functools

import jax
import jax.numpy as jnp
from jax import lax
from jax.experimental import pallas as pl
from jax.experimental.pallas import tpu as pltpu
from jax.sharding import Mesh
from jax.sharding import PartitionSpec as P

ROW = ("y_hi", "x", "core")
COL = ("y_lo", "z")
AHEAD = 2


def shift(value, axis, size, by):
    return lax.ppermute(value, axis, [(i, (i + by) % size) for i in range(size)])


def multiply(origins, tokens_ref, *refs):
    y_hi, x, core = (lax.axis_index(name) for name in ROW)
    y_lo = lax.axis_index("y_lo")
    weights, hidden, tokens, held, gate, up, token_sem, weight_sem = refs[:16], *refs[16:]
    parts = len(weights) // 2
    depth = tokens_ref.shape[2]

    def token_copy(r, half):
        flip, offset = origins[r]
        from_core = core if half == 0 else 1 - core
        from_z = 2 * lax.rem(x + offset, 4) + from_core
        from_y = lax.rem(y_hi + flip + y_lo, 2)
        return pltpu.make_async_copy(
            tokens_ref.at[2 * from_z + from_y],
            tokens.at[r, :, pl.ds(half * depth, depth)],
            token_sem.at[r, half],
        )

    def weight_copy(r, half):
        return pltpu.make_async_copy(
            weights[2 * r + half],
            held.at[r, :, pl.ds(half * depth, depth), :],
            weight_sem.at[r, half],
        )

    def start(r):
        for half in range(2):
            token_copy(r, half).start()
            weight_copy(r, half).start()

    for r in range(AHEAD):
        start(r)
    for r in range(parts):
        for half in range(2):
            token_copy(r, half).wait()
            weight_copy(r, half).wait()
        if r + AHEAD < parts:
            start(r + AHEAD)
        gate_part = jnp.dot(tokens[r], held[r, 0], preferred_element_type=jnp.float32)
        up_part = jnp.dot(tokens[r], held[r, 1], preferred_element_type=jnp.float32)
        if r == 0:
            gate[...] = gate_part
            up[...] = up_part
        else:
            gate[...] += gate_part
            up[...] += up_part
    value = gate[...]
    hidden[...] = value / (1.0 + jnp.exp(-value)) * up[...]


def per_device(tokens, gate_weight, up_weight):
    rows, depth = tokens.shape
    width = gate_weight.shape[1]

    own = jnp.stack([gate_weight, up_weight])
    own, tokens = lax.optimization_barrier((own, tokens))
    other_tokens = shift(tokens, "y_lo", 2, 1)
    across = shift(own, "y_hi", 2, 1)
    own_1 = shift(own, "x", 4, 1)
    own_3 = shift(own, "x", 4, -1)
    own_2g = shift(own_1[0], "x", 4, 1)
    own_2u = shift(own_3[1], "x", 4, -1)
    own_2 = jnp.stack([own_2g, own_2u])
    pair = jnp.stack([tokens, other_tokens])
    gathered = lax.all_gather(pair, "z", axis=0, tiled=True)
    across_1 = shift(across, "x", 4, 1)
    across_3 = shift(across, "x", 4, -1)
    across_2 = shift(own_2, "y_hi", 2, 1)

    blocks = [
        (0, 0, own),
        (0, 3, own_1),
        (0, 1, own_3),
        (0, 2, own_2),
        (1, 0, across),
        (1, 3, across_1),
        (1, 1, across_3),
        (1, 2, across_2),
    ]
    weights = []
    for _, _, block in blocks:
        weights += [block, shift(block, "core", 2, 1)]
    origins = tuple((flip, offset) for flip, offset, _ in blocks)
    parts = len(blocks)
    anywhere = pl.BlockSpec(memory_space=pl.ANY)
    return pl.pallas_call(
        functools.partial(multiply, origins),
        out_shape=jax.ShapeDtypeStruct((rows, width), jnp.float32),
        in_specs=[anywhere] * (1 + 2 * parts),
        out_specs=pl.BlockSpec(memory_space=pltpu.VMEM),
        scratch_shapes=[
            pltpu.VMEM((parts, rows, 2 * depth), tokens.dtype),
            pltpu.VMEM((parts, 2, 2 * depth, width), gate_weight.dtype),
            pltpu.VMEM((rows, width), jnp.float32),
            pltpu.VMEM((rows, width), jnp.float32),
            pltpu.SemaphoreType.DMA((parts, 2)),
            pltpu.SemaphoreType.DMA((parts, 2)),
        ],
        compiler_params=pltpu.CompilerParams(vmem_limit_bytes=58 * 1024 * 1024),
        cost_estimate=pl.CostEstimate(
            flops=4 * rows * width * depth * 16,
            bytes_accessed=2 * depth * 16 * (rows + 2 * width) + 4 * rows * width,
            transcendentals=rows * width,
        ),
    )(gathered, *weights)


def solution(mesh):
    fine = Mesh(mesh.devices.reshape(2, 4, 2, 2, 8), ROW + COL)
    spec = P(ROW, COL)
    return jax.shard_map(
        per_device, mesh=fine, in_specs=(spec,) * 3, out_specs=spec, check_vma=False
    )
```

```python
import functools

import jax
import jax.numpy as jnp
from jax import lax
from jax.experimental import pallas as pl
from jax.experimental.pallas import tpu as pltpu
from jax.sharding import Mesh
from jax.sharding import PartitionSpec as P

ROW = ("y_hi", "x", "core")
COL = ("y_lo", "z")
AHEAD = 2


def shift(value, axis, size, by):
    return lax.ppermute(value, axis, [(i, (i + by) % size) for i in range(size)])


def after(waits, *values):
    waits, values = lax.optimization_barrier((tuple(waits), tuple(values)))
    return values


def multiply(origins, tokens_ref, *refs):
    y_hi, x, core = (lax.axis_index(name) for name in ROW)
    y_lo = lax.axis_index("y_lo")
    weights, hidden, tokens, held, gate, up, token_sem, weight_sem = refs[:16], *refs[16:]
    parts = len(weights) // 2
    depth = tokens_ref.shape[2]

    def token_copy(r, half):
        flip, offset = origins[r]
        from_core = core if half == 0 else 1 - core
        from_z = 2 * lax.rem(x + offset, 4) + from_core
        from_y = lax.rem(y_hi + flip + y_lo, 2)
        return pltpu.make_async_copy(
            tokens_ref.at[2 * from_z + from_y],
            tokens.at[r, :, pl.ds(half * depth, depth)],
            token_sem.at[r, half],
        )

    def weight_copy(r, half):
        return pltpu.make_async_copy(
            weights[2 * r + half],
            held.at[r, :, pl.ds(half * depth, depth), :],
            weight_sem.at[r, half],
        )

    def start(r):
        for half in range(2):
            token_copy(r, half).start()
            weight_copy(r, half).start()

    for r in range(AHEAD):
        start(r)
    for r in range(parts):
        for half in range(2):
            token_copy(r, half).wait()
            weight_copy(r, half).wait()
        if r + AHEAD < parts:
            start(r + AHEAD)
        gate_part = jnp.dot(tokens[r], held[r, 0], preferred_element_type=jnp.float32)
        up_part = jnp.dot(tokens[r], held[r, 1], preferred_element_type=jnp.float32)
        if r == 0:
            gate[...] = gate_part
            up[...] = up_part
        else:
            gate[...] += gate_part
            up[...] += up_part
    value = gate[...]
    hidden[...] = value / (1.0 + jnp.exp(-value)) * up[...]


def per_device(tokens, gate_weight, up_weight):
    rows, depth = tokens.shape
    width = gate_weight.shape[1]

    own = jnp.stack([gate_weight, up_weight])
    own, tokens = lax.optimization_barrier((own, tokens))
    other_tokens = shift(tokens, "y_lo", 2, 1)
    across = shift(own, "y_hi", 2, 1)
    own_1 = shift(own, "x", 4, 1)
    own_3 = shift(own, "x", 4, -1)
    own_2g = shift(own_1[0], "x", 4, 1)
    own_2u = shift(own_3[1], "x", 4, -1)
    own_2 = jnp.stack([own_2g, own_2u])
    pair = jnp.stack([tokens, other_tokens])
    gathered = lax.all_gather(pair, "z", axis=0, tiled=True)
    (across_late,) = after([own_2g, own_2u], across)
    across_1 = shift(across_late, "x", 4, 1)
    across_3 = shift(across_late, "x", 4, -1)
    across_2 = shift(own_2, "y_hi", 2, 1)

    blocks = [
        (0, 0, own),
        (0, 3, own_1),
        (0, 1, own_3),
        (0, 2, own_2),
        (1, 0, across),
        (1, 3, across_1),
        (1, 1, across_3),
        (1, 2, across_2),
    ]
    weights = []
    for _, _, block in blocks:
        weights += [block, shift(block, "core", 2, 1)]
    origins = tuple((flip, offset) for flip, offset, _ in blocks)
    parts = len(blocks)
    anywhere = pl.BlockSpec(memory_space=pl.ANY)
    return pl.pallas_call(
        functools.partial(multiply, origins),
        out_shape=jax.ShapeDtypeStruct((rows, width), jnp.float32),
        in_specs=[anywhere] * (1 + 2 * parts),
        out_specs=pl.BlockSpec(memory_space=pltpu.VMEM),
        scratch_shapes=[
            pltpu.VMEM((parts, rows, 2 * depth), tokens.dtype),
            pltpu.VMEM((parts, 2, 2 * depth, width), gate_weight.dtype),
            pltpu.VMEM((rows, width), jnp.float32),
            pltpu.VMEM((rows, width), jnp.float32),
            pltpu.SemaphoreType.DMA((parts, 2)),
            pltpu.SemaphoreType.DMA((parts, 2)),
        ],
        compiler_params=pltpu.CompilerParams(vmem_limit_bytes=58 * 1024 * 1024),
        cost_estimate=pl.CostEstimate(
            flops=4 * rows * width * depth * 16,
            bytes_accessed=2 * depth * 16 * (rows + 2 * width) + 4 * rows * width,
            transcendentals=rows * width,
        ),
    )(gathered, *weights)


def solution(mesh):
    fine = Mesh(mesh.devices.reshape(2, 4, 2, 2, 8), ROW + COL)
    spec = P(ROW, COL)
    return jax.shard_map(
        per_device, mesh=fine, in_specs=(spec,) * 3, out_specs=spec, check_vma=False
    )
```

```python
import functools

import jax
import jax.numpy as jnp
from jax import lax
from jax.experimental import pallas as pl
from jax.experimental.pallas import tpu as pltpu
from jax.sharding import Mesh
from jax.sharding import PartitionSpec as P

ROW = ("y_hi", "x", "core")
COL = ("y_lo", "z")
AHEAD = 2


def shift(value, axis, size, by):
    return lax.ppermute(value, axis, [(i, (i + by) % size) for i in range(size)])


def after(waits, *values):
    waits, values = lax.optimization_barrier((tuple(waits), tuple(values)))
    return values


def multiply(origins, tokens_ref, *refs):
    y_hi, x, core = (lax.axis_index(name) for name in ROW)
    y_lo = lax.axis_index("y_lo")
    weights, refs = refs[:16], refs[16:]
    hidden, tokens, held, gate, up, token_sem, weight_sem, write_sem = refs
    parts = len(weights) // 2
    depth = tokens_ref.shape[2]

    def token_copy(r, half):
        flip, offset = origins[r]
        from_core = core if half == 0 else 1 - core
        from_z = 2 * lax.rem(x + offset, 4) + from_core
        from_y = lax.rem(y_hi + flip + y_lo, 2)
        return pltpu.make_async_copy(
            tokens_ref.at[2 * from_z + from_y],
            tokens.at[r, :, pl.ds(half * depth, depth)],
            token_sem.at[r, half],
        )

    def weight_copy(r, half):
        return pltpu.make_async_copy(
            weights[2 * r + half],
            held.at[r, :, pl.ds(half * depth, depth), :],
            weight_sem.at[r, half],
        )

    def start(r):
        for half in range(2):
            token_copy(r, half).start()
            weight_copy(r, half).start()

    for r in range(AHEAD):
        start(r)
    for r in range(parts):
        for half in range(2):
            token_copy(r, half).wait()
            weight_copy(r, half).wait()
        if r + AHEAD < parts:
            start(r + AHEAD)
        if r < parts - 1:
            gate_part = jnp.dot(tokens[r], held[r, 0], preferred_element_type=jnp.float32)
            up_part = jnp.dot(tokens[r], held[r, 1], preferred_element_type=jnp.float32)
            if r == 0:
                gate[...] = gate_part
                up[...] = up_part
            else:
                gate[...] += gate_part
                up[...] += up_part
    last, tile = parts - 1, 128
    writes = []
    for at in range(0, gate.shape[0], tile):
        rows = slice(at, at + tile)
        left = tokens[last, rows, :]
        value = gate[rows, :] + jnp.dot(
            left, held[last, 0], preferred_element_type=jnp.float32
        )
        times = up[rows, :] + jnp.dot(
            left, held[last, 1], preferred_element_type=jnp.float32
        )
        gate[rows, :] = value / (1.0 + jnp.exp(-value)) * times
        few = pl.ds(at, tile)
        write = pltpu.make_async_copy(
            gate.at[few, :], hidden.at[few, :], write_sem.at[at // tile]
        )
        write.start()
        writes.append(write)
    for write in writes:
        write.wait()


def per_device(tokens, gate_weight, up_weight):
    rows, depth = tokens.shape
    width = gate_weight.shape[1]

    own = jnp.stack([gate_weight, up_weight])
    other_tokens = shift(tokens, "y_lo", 2, 1)
    own, other_tokens = lax.optimization_barrier((own, other_tokens))
    across = shift(own, "y_hi", 2, 1)
    own_1 = shift(own, "x", 4, 1)
    own_3 = shift(own, "x", 4, -1)
    own_2g = shift(own_1[0], "x", 4, 1)
    own_2u = shift(own_3[1], "x", 4, -1)
    own_2 = jnp.stack([own_2g, own_2u])
    pair = jnp.stack([tokens, other_tokens])
    gathered = lax.all_gather(pair, "z", axis=0, tiled=True)
    (across_late,) = after([own_2g, own_2u], across)
    across_1 = shift(across_late, "x", 4, 1)
    across_3 = shift(across_late, "x", 4, -1)
    across_2 = shift(own_2, "y_hi", 2, 1)

    blocks = [
        (0, 0, own),
        (0, 3, own_1),
        (0, 1, own_3),
        (0, 2, own_2),
        (1, 0, across),
        (1, 3, across_1),
        (1, 1, across_3),
        (1, 2, across_2),
    ]
    weights = []
    for _, _, block in blocks:
        weights += [block, shift(block, "core", 2, 1)]
    origins = tuple((flip, offset) for flip, offset, _ in blocks)
    parts = len(blocks)
    anywhere = pl.BlockSpec(memory_space=pl.ANY)
    return pl.pallas_call(
        functools.partial(multiply, origins),
        out_shape=jax.ShapeDtypeStruct((rows, width), jnp.float32),
        in_specs=[anywhere] * (1 + 2 * parts),
        out_specs=anywhere,
        scratch_shapes=[
            pltpu.VMEM((parts, rows, 2 * depth), tokens.dtype),
            pltpu.VMEM((parts, 2, 2 * depth, width), gate_weight.dtype),
            pltpu.VMEM((rows, width), jnp.float32),
            pltpu.VMEM((rows, width), jnp.float32),
            pltpu.SemaphoreType.DMA((parts, 2)),
            pltpu.SemaphoreType.DMA((parts, 2)),
            pltpu.SemaphoreType.DMA((rows // 128,)),
        ],
        compiler_params=pltpu.CompilerParams(vmem_limit_bytes=58 * 1024 * 1024),
        cost_estimate=pl.CostEstimate(
            flops=4 * rows * width * depth * 16,
            bytes_accessed=2 * depth * 16 * (rows + 2 * width) + 4 * rows * width,
            transcendentals=rows * width,
        ),
    )(gathered, *weights)


def solution(mesh):
    fine = Mesh(mesh.devices.reshape(2, 4, 2, 2, 8), ROW + COL)
    spec = P(ROW, COL)
    return jax.shard_map(
        per_device, mesh=fine, in_specs=(spec,) * 3, out_specs=spec, check_vma=False
    )
```

```python
import functools

import jax
import jax.numpy as jnp
from jax import lax
from jax.experimental import pallas as pl
from jax.experimental.pallas import tpu as pltpu
from jax.sharding import Mesh
from jax.sharding import PartitionSpec as P

ROW = ("y_hi", "x", "core")
COL = ("y_lo", "z")
AHEAD = 2


def shift(value, axis, size, by):
    return lax.ppermute(value, axis, [(i, (i + by) % size) for i in range(size)])


def after(waits, *values):
    waits, values = lax.optimization_barrier((tuple(waits), tuple(values)))
    return values


def multiply(origins, tokens_ref, *refs):
    y_hi, x, core = (lax.axis_index(name) for name in ROW)
    y_lo = lax.axis_index("y_lo")
    weights, refs = refs[:16], refs[16:]
    hidden, tokens, held, gate, up, token_sem, weight_sem, write_sem = refs
    parts = len(weights) // 2
    depth = tokens_ref.shape[2]

    def token_copy(r, half):
        flip, offset = origins[r]
        from_core = core if half == 0 else 1 - core
        from_z = 2 * lax.rem(x + offset, 4) + from_core
        from_y = lax.rem(y_hi + flip + y_lo, 2)
        return pltpu.make_async_copy(
            tokens_ref.at[2 * from_z + from_y],
            tokens.at[r, :, pl.ds(half * depth, depth)],
            token_sem.at[r, half],
        )

    def weight_copy(r, half):
        return pltpu.make_async_copy(
            weights[2 * r + half],
            held.at[r, :, pl.ds(half * depth, depth), :],
            weight_sem.at[r, half],
        )

    def start(r):
        for half in range(2):
            token_copy(r, half).start()
            weight_copy(r, half).start()

    for r in range(AHEAD):
        start(r)
    for r in range(parts):
        for half in range(2):
            token_copy(r, half).wait()
            weight_copy(r, half).wait()
        if r + AHEAD < parts:
            start(r + AHEAD)
        if r < parts - 1:
            gate_part = jnp.dot(tokens[r], held[r, 0], preferred_element_type=jnp.float32)
            up_part = jnp.dot(tokens[r], held[r, 1], preferred_element_type=jnp.float32)
            if r == 0:
                gate[...] = gate_part
                up[...] = up_part
            else:
                gate[...] += gate_part
                up[...] += up_part
    last, tile = parts - 1, 128
    writes = []
    for at in range(0, gate.shape[0], tile):
        rows = slice(at, at + tile)
        left = tokens[last, rows, :]
        value = gate[rows, :] + jnp.dot(
            left, held[last, 0], preferred_element_type=jnp.float32
        )
        times = up[rows, :] + jnp.dot(
            left, held[last, 1], preferred_element_type=jnp.float32
        )
        gate[rows, :] = value / (1.0 + jnp.exp(-value)) * times
        few = pl.ds(at, tile)
        write = pltpu.make_async_copy(
            gate.at[few, :], hidden.at[few, :], write_sem.at[at // tile]
        )
        write.start()
        writes.append(write)
    for write in writes:
        write.wait()


def per_device(tokens, gate_weight, up_weight):
    rows, depth = tokens.shape
    width = gate_weight.shape[1]

    own = jnp.stack([gate_weight, up_weight])
    other_tokens = shift(tokens, "y_lo", 2, 1)
    room = jnp.zeros((2, rows, depth), tokens.dtype)
    room = lax.dynamic_update_slice(room, tokens[None], (0, 0, 0))
    own, room, other_tokens = lax.optimization_barrier((own, room, other_tokens))
    across = shift(own, "y_hi", 2, 1)
    own_1 = shift(own, "x", 4, 1)
    own_3 = shift(own, "x", 4, -1)
    own_2g = shift(own_1[0], "x", 4, 1)
    own_2u = shift(own_3[1], "x", 4, -1)
    own_2 = jnp.stack([own_2g, own_2u])
    pair = lax.dynamic_update_slice(room, other_tokens[None], (1, 0, 0))
    gathered = lax.all_gather(pair, "z", axis=0, tiled=True)
    (across_late,) = after([own_2u], across)
    across_1 = shift(across_late, "x", 4, 1)
    across_3 = shift(across_late, "x", 4, -1)
    across_2 = shift(own_2, "y_hi", 2, 1)

    blocks = [
        (0, 0, own),
        (0, 3, own_1),
        (0, 1, own_3),
        (0, 2, own_2),
        (1, 0, across),
        (1, 3, across_1),
        (1, 1, across_3),
        (1, 2, across_2),
    ]
    weights = []
    for _, _, block in blocks:
        weights += [block, shift(block, "core", 2, 1)]
    origins = tuple((flip, offset) for flip, offset, _ in blocks)
    parts = len(blocks)
    anywhere = pl.BlockSpec(memory_space=pl.ANY)
    return pl.pallas_call(
        functools.partial(multiply, origins),
        out_shape=jax.ShapeDtypeStruct((rows, width), jnp.float32),
        in_specs=[anywhere] * (1 + 2 * parts),
        out_specs=anywhere,
        scratch_shapes=[
            pltpu.VMEM((parts, rows, 2 * depth), tokens.dtype),
            pltpu.VMEM((parts, 2, 2 * depth, width), gate_weight.dtype),
            pltpu.VMEM((rows, width), jnp.float32),
            pltpu.VMEM((rows, width), jnp.float32),
            pltpu.SemaphoreType.DMA((parts, 2)),
            pltpu.SemaphoreType.DMA((parts, 2)),
            pltpu.SemaphoreType.DMA((rows // 128,)),
        ],
        compiler_params=pltpu.CompilerParams(vmem_limit_bytes=58 * 1024 * 1024),
        cost_estimate=pl.CostEstimate(
            flops=4 * rows * width * depth * 16,
            bytes_accessed=2 * depth * 16 * (rows + 2 * width) + 4 * rows * width,
            transcendentals=rows * width,
        ),
    )(gathered, *weights)


def solution(mesh):
    fine = Mesh(mesh.devices.reshape(2, 4, 2, 2, 8), ROW + COL)
    spec = P(ROW, COL)
    return jax.shard_map(
        per_device, mesh=fine, in_specs=(spec,) * 3, out_specs=spec, check_vma=False
    )
```
